256 devices in a mesh: dp: 8 (over x, core), expert: 32 (over z, y).
Axes of the slice: x: 4, y: 4, z: 8, core: 2. Of those that a mesh axis runs over, the one named last changes fastest.
Arguments:
- tokens: bfloat16 [8192, 7168], P('expert', 'dp'), may hold values from -6 to 6
- grad_out: bfloat16 [8192, 7168], P('expert', 'dp'), may hold values from -6 to 6
- route_ids: int32 [8192, 8], P('expert'), may hold values from 0 to 255, all different within a row; in each aligned block of 256 rows (0 to 255, 256 to 511, ...) at most 12 rows name the same one
- route_gates: float32 [8192, 8], P('expert'), may hold values from 0.1 to 1
- w_gate: bfloat16 [32, 7168, 1024], P('expert', 'dp'), may hold values from -0.0625 to 0.0625
- w_up: bfloat16 [32, 7168, 1024], P('expert', 'dp'), may hold values from -0.0625 to 0.0625
- w_down: bfloat16 [32, 1024, 7168], P('expert', None, 'dp'), may hold values from -0.1875 to 0.1875
- shared_gate: bfloat16 [7168, 1024], P('dp', 'expert'), may hold values from -0.0625 to 0.0625
- shared_up: bfloat16 [7168, 1024], P('dp', 'expert'), may hold values from -0.0625 to 0.0625
- shared_down: bfloat16 [1024, 7168], P('expert', 'dp'), may hold values from -0.1875 to 0.1875
Outputs:
- grad_tokens: bfloat16 [8192, 7168], P('expert', 'dp')
- grad_gate: bfloat16 [32, 7168, 1024], P('expert', 'dp')
- grad_up: bfloat16 [32, 7168, 1024], P('expert', 'dp')
- grad_down: bfloat16 [32, 1024, 7168], P('expert', None, 'dp')
- grad_shared_gate: float32 [7168, 1024], P('dp', 'expert')
- grad_shared_up: float32 [7168, 1024], P('dp', 'expert')
- grad_shared_down: float32 [1024, 7168], P('expert', 'dp')
The draws below stay inside these ranges and needn't reach their ends.
Inputs may be any that keep to these rules, and one draw needn't show every extreme that they name: `route_ids`: each row names 8 different experts; in each aligned block of 256 rows no expert is named by more than 12 rows, a bound that some block reaches.
All inputs are finite; a program needn't handle non-finite values.
Results may differ from the reference program's by a relative error of at most 0.018.
Values may be sent and summed in bfloat16 or wider, within the bound.
No kernel may reach another device: no remote copies, remote signals or barrier semaphores. Data moves between devices by JAX's collectives and lax.ppermute only.
A program may use at most 128 MiB of HBM per device.

```python
import math
import jax
import jax.numpy as jnp
import numpy as np
from jax import lax

D = 7168
HID = 1024
HSH = 1024
ALL_EXP = 256
TOPK = 8
TOK_DEV = 256
EXPERTS = 32
TOKENS = 8192
CAP = 12
N_EXPERT = 32


def block_levels(own_key, shape, split, low, high):
    loudness, own = 1.0, jax.random.fold_in(own_key, 6)
    for dim, parts in split:
        heights = jnp.exp(jax.random.uniform(jax.random.fold_in(own, dim), (parts,), jnp.float32, low / len(split), high / len(split)))
        loudness = loudness * jnp.repeat(heights, shape[dim] // parts).reshape([-1 if axis == dim else 1 for axis in range(len(shape))])
    return loudness


def routed_block(rng, own, number, rows, count, top, limit, skew):
    sequence = jax.random.permutation(rng, count)
    heavy_load, ordinary = shares(count, rows * top, limit, skew, True), shares(count, rows * top, limit, skew, False)
    places = jnp.arange(count)

    def named(lengths, rotation):
        used = int((lengths > 0).sum())
        fixed = max(1, used // 4)
        moved = fixed + (places - fixed + rotation * (used - fixed)) % max(1, count - fixed)
        return jnp.zeros((count,), jnp.int32).at[sequence[jnp.where(places < fixed, places, moved)]].set(jnp.asarray(lengths, jnp.int32))

    lengths = jnp.where(number % 4 == 0, named(heavy_load, number // 4), named(ordinary, number - number // 4 - 1))
    mixed = jax.random.permutation(jax.random.fold_in(own, 3), count)
    donor, receiver = mixed[0:count // 2 * 2:2], mixed[1:count // 2 * 2:2]
    room = jnp.minimum(lengths[donor] - 1, limit - lengths[receiver]) // 2
    room = jnp.where((donor == sequence[0]) | (receiver == sequence[0]) | (lengths[receiver] == 0), 0, jnp.maximum(room, 0))
    moved = jax.random.randint(jax.random.fold_in(own, 4), (count // 2,), 0, 1 << 20) % (room + 1)
    lengths = lengths.at[donor].add(-moved).at[receiver].add(moved)
    members = jnp.searchsorted(jnp.cumsum(lengths), jnp.arange(rows * top), side="right").astype(jnp.int32)
    table = members.reshape(top, rows).T
    table = table[jax.random.permutation(jax.random.fold_in(own, 1), rows)]
    rotation = jax.random.randint(jax.random.fold_in(own, 2), (rows, 1), 0, top)
    return jnp.take_along_axis(table, (jnp.arange(top)[None, :] + rotation) % top, axis=1)


def shares(number_of, total, reach, skew, full):
    weights = [(1 << 20) // math.isqrt(standing ** skew) + 1 for standing in range(1, number_of + 1)]
    largest = reach if full else min(reach, max(-(-total // number_of), total * weights[0] // sum(weights)))
    least = 1 if total - largest >= number_of - 1 else 0
    given, surplus = [largest] + [least] * (number_of - 1), total - largest - least * (number_of - 1)
    while surplus > 0:
        movable = [i for i in range(1, number_of) if given[i] < largest] or [i for i in range(1, number_of) if given[i] < reach]
        mass, budget = sum([weights[i] for i in movable]), surplus
        for i in movable:
            addition = min(reach - given[i], max(1, budget * weights[i] // mass), surplus)
            given[i] = given[i] + addition
            surplus = surplus - addition
    return np.array(given)


def gaussian(rng, dims, deviation, limit, split=(), kind=jnp.bfloat16):
    array = jax.random.normal(rng, dims, jnp.float32) * deviation
    if len(split) > 0:
        array = block_levels(rng, dims, split, -0.22, 0.18) * array
    return jnp.clip(array, min=-limit, max=limit).astype(kind)


def setup_inputs(seed: int = 0) -> dict:
    arg_keys = jax.random.split(jax.random.key(seed), 11)
    tokens = gaussian(arg_keys[0], (TOKENS, D), 1.0, 6.0, ((0, 32), (1, 8)))
    grad_out = gaussian(arg_keys[1], (TOKENS, D), 1.0, 6.0, ((0, 32), (1, 8)))
    route_ids_keys = jax.random.split(jax.random.fold_in(arg_keys[2], 1), TOKENS // TOK_DEV)
    route_ids_turns = jax.random.permutation(jax.random.fold_in(arg_keys[2], 3), TOKENS // TOK_DEV)
    route_ids = jax.vmap(lambda own, number: routed_block(jax.random.fold_in(arg_keys[2], 2), own, number, TOK_DEV, ALL_EXP, TOPK, CAP, 2))(route_ids_keys, route_ids_turns).reshape((TOKENS, TOPK))
    route_gates = jnp.clip(jnp.exp(math.log(1.0) - 2.3025851 * jax.random.uniform(arg_keys[3], (TOKENS, TOPK), jnp.float32) ** block_levels(arg_keys[3], (TOKENS, TOPK), ((0, 32),), -0.2, 0.2)), 0.1, 1.0)
    w_gate = gaussian(arg_keys[4], (EXPERTS, D, HID), D ** -0.5, 0.0625, ((0, 32), (1, 8)))
    w_up = gaussian(arg_keys[5], (EXPERTS, D, HID), D ** -0.5, 0.0625, ((0, 32), (1, 8)))
    w_down = gaussian(arg_keys[6], (EXPERTS, HID, D), HID ** -0.5, 0.1875, ((0, 32), (2, 8)))
    shared_gate = gaussian(arg_keys[7], (D, HSH), D ** -0.5, 0.0625, ((0, 8), (1, 32)))
    shared_up = gaussian(arg_keys[8], (D, HSH), D ** -0.5, 0.0625, ((0, 8), (1, 32)))
    shared_down = gaussian(arg_keys[9], (HSH, D), HSH ** -0.5, 0.1875, ((0, 32), (1, 8)))
    return dict(tokens=tokens, grad_out=grad_out, route_ids=route_ids, route_gates=route_gates, w_gate=w_gate, w_up=w_up, w_down=w_down, shared_gate=shared_gate, shared_up=shared_up, shared_down=shared_down)


def silu_parts(pre):
    sigmoid_val = jax.nn.sigmoid(pre)
    return pre * sigmoid_val, sigmoid_val * (1.0 + pre * (1.0 - sigmoid_val))


def contract_rows(left, right):
    return lax.dot_general(left, right, (((0,), (0,)), ((), ())), preferred_element_type=jnp.float32)


def contract_cols(left, right):
    return lax.dot_general(left, right, (((1,), (1,)), ((), ())), preferred_element_type=jnp.float32)


def expert_terms(rows_in, rows_grad, weight_gate, weight_up, weight_down):
    pre_gate = jnp.dot(rows_in, weight_gate, preferred_element_type=jnp.float32)
    pre_up = jnp.dot(rows_in, weight_up, preferred_element_type=jnp.float32)
    grad_act = contract_cols(rows_grad, weight_down)
    silu_val, silu_slope = silu_parts(pre_gate)
    activated = (silu_val * pre_up).astype(jnp.bfloat16)
    grad_gate_pre = (grad_act * pre_up * silu_slope).astype(jnp.bfloat16)
    grad_up_pre = (grad_act * silu_val).astype(jnp.bfloat16)
    back = contract_cols(grad_gate_pre, weight_gate) + contract_cols(grad_up_pre, weight_up)
    return (contract_rows(rows_in, grad_gate_pre), contract_rows(rows_in, grad_up_pre),
            contract_rows(activated, rows_grad), back)


def settle(value):
    return lax.optimization_barrier(value.astype(jnp.bfloat16)).astype(jnp.float32)


def reference(tokens, grad_out, route_ids, route_gates, w_gate, w_up, w_down, shared_gate, shared_up, shared_down):
    grad_scale = 1.0 / N_EXPERT
    row_count = N_EXPERT * CAP
    order_base = jnp.arange(TOKENS, dtype=jnp.int32)

    def one_expert(carry, expert_id):
        matches = route_ids == expert_id
        chosen = jnp.any(matches, axis=1)
        gate_total = jnp.sum(jnp.where(matches, route_gates, jnp.zeros_like(route_gates)), axis=1)
        sort_key = jnp.where(chosen, 0, TOKENS).astype(jnp.int32) + order_base
        picked = jnp.argsort(sort_key)[:row_count].astype(jnp.int32)
        rows_in = tokens[picked]
        rows_grad = (gate_total[picked][:, None] * grad_out[picked].astype(jnp.float32)).astype(jnp.bfloat16)
        part_gate, part_up, part_down, back = expert_terms(rows_in, rows_grad, w_gate[expert_id], w_up[expert_id], w_down[expert_id])
        carry = carry.at[picked].add(settle(back))
        return carry, ((part_gate * grad_scale).astype(jnp.bfloat16), (part_up * grad_scale).astype(jnp.bfloat16),
                       (part_down * grad_scale).astype(jnp.bfloat16))

    routed, (grad_gate, grad_up, grad_down) = lax.scan(
        one_expert, jnp.zeros((TOKENS, D), jnp.float32), jnp.arange(EXPERTS, dtype=jnp.int32))

    groups_in = tokens.reshape(N_EXPERT, TOK_DEV, D)
    groups_grad = grad_out.reshape(N_EXPERT, TOK_DEV, D)

    def one_group(carry, pair):
        rows_in, rows_grad = pair
        part_gate, part_up, part_down, back = expert_terms(rows_in, rows_grad, shared_gate, shared_up, shared_down)
        return (carry[0] + part_gate, carry[1] + part_up, carry[2] + part_down), back

    start = (jnp.zeros((D, HSH), jnp.float32), jnp.zeros((D, HSH), jnp.float32), jnp.zeros((HSH, D), jnp.float32))
    (sum_gate, sum_up, sum_down), shared_back = lax.scan(one_group, start, (groups_in, groups_grad))
    grad_tokens = (shared_back.reshape(TOKENS, D) + routed).astype(jnp.bfloat16)
    return (grad_tokens, grad_gate, grad_up, grad_down,
            sum_gate * grad_scale, sum_up * grad_scale, sum_down * grad_scale)
```

```python
import jax
import jax.numpy as jnp
from jax import lax
from jax.sharding import Mesh
from jax.sharding import PartitionSpec as P

CAP = 12
NY = 4
BF16 = jnp.bfloat16
F32 = jnp.float32


def silu_parts(pre):
    sigmoid_val = jax.nn.sigmoid(pre)
    return (pre * sigmoid_val, sigmoid_val * (1.0 + pre * (1.0 - sigmoid_val)))


def dot_rows(left, right):
    return lax.dot_general(left, right, (((0,), (0,)), ((), ())), preferred_element_type=F32)


def dot_cols(left, right):
    return lax.dot_general(left, right, (((1,), (1,)), ((), ())), preferred_element_type=F32)


def dot(left, right):
    return jnp.dot(left, right, preferred_element_type=F32)


def hidden_products(part_gate, part_up, part_act):
    silu_val, silu_slope = silu_parts(part_gate)
    activated = (silu_val * part_up).astype(BF16)
    grad_gate_pre = (part_act * part_up * silu_slope).astype(BF16)
    grad_up_pre = (part_act * silu_val).astype(BF16)
    return (activated, grad_gate_pre, grad_up_pre)


def shift(value, axis, by):
    size = lax.axis_size(axis)
    return lax.ppermute(value, axis, [(i, (i + by) % size) for i in range(size)])


def own_blocks(rows):
    n_x, n_core = lax.axis_size("x"), lax.axis_size("core")
    block = rows // (n_x * n_core)
    place = jnp.arange(rows, dtype=jnp.int32)
    half, rest = place // (n_x * block), place % (n_x * block)
    spot, row = rest // block, rest % block
    natural_half = (half + lax.axis_index("core")) % n_core
    natural_spot = (spot + lax.axis_index("x")) % n_x
    return (natural_half * n_x + natural_spot) * block + row


def one_hot(source, columns):
    return (source[:, None] == jnp.arange(columns, dtype=jnp.int32)[None, :]).astype(BF16)


def reduce_rows(part):
    n_x = lax.axis_size("x")
    rows, cols = part.shape
    half = rows // 2
    got = shift(part[half:].astype(BF16), "core", 1)
    summed = (part[:half] + got.astype(F32)).reshape(n_x, half // n_x, cols)
    total = summed[0]
    pieces = [shift(summed[j].astype(BF16), "x", j) for j in range(1, n_x)]
    for piece in pieces:
        total = total + piece.astype(F32)
    return total


def gather_rows(value):
    n_x = lax.axis_size("x")
    half = jnp.concatenate([value] + [shift(value, "x", -j) for j in range(1, n_x)], axis=0)
    return jnp.concatenate([half, shift(half, "core", 1)], axis=0)


def shards(tokens, grad_out, route_ids, route_gates, w_gate, w_up, w_down, shared_gate, shared_up, shared_down):
    n_z, n_y, n_x = lax.axis_size("z"), lax.axis_size("y"), lax.axis_size("x")
    n_exp = n_z * n_y
    scale = 1.0 / n_exp
    n_tok, width = tokens.shape
    hid = w_gate.shape[2]
    units = shared_down.shape[0]

    own_w = jnp.concatenate([shared_gate.T, shared_up.T, shared_down], axis=0)
    all_w = lax.all_gather(own_w, "z", axis=0, tiled=True)

    tok_order = own_blocks(n_tok)
    tok_perm = one_hot(tok_order, n_tok)
    tok_own = dot(tok_perm, tokens).astype(BF16)
    grd_own = dot(tok_perm, grad_out).astype(BF16)

    targets = jnp.arange(n_exp, dtype=jnp.int32)
    matches = route_ids[:, :, None] == targets[None, None, :]
    chosen = jnp.any(matches, axis=1).astype(jnp.int32)
    gate_total = jnp.sum(jnp.where(matches, route_gates[:, :, None], 0.0), axis=1)
    slot_rank = jnp.cumsum(chosen, axis=0) - 1
    slot_ids = jnp.arange(CAP, dtype=jnp.int32)
    placement = (chosen[:, :, None] == 1) & (slot_rank[:, :, None] == slot_ids[None, None, :])
    place_bf = placement.astype(BF16)
    send_in = jnp.einsum("tec,td->ecd", place_bf, tokens, preferred_element_type=F32).astype(BF16)
    slot_gate = jnp.einsum("tec,te->ec", placement.astype(F32), gate_total, precision=lax.Precision.HIGHEST)
    picked_grad = jnp.einsum("tec,td->ecd", place_bf, grad_out, preferred_element_type=F32)
    send_grad = (slot_gate[:, :, None] * picked_grad).astype(BF16)
    send = jnp.concatenate([send_in, send_grad], axis=1)
    recv = lax.all_to_all(send, ("z", "y"), split_axis=0, concat_axis=0, tiled=True)

    tok_all = [tok_own] + [shift(tok_own, "y", j) for j in range(1, n_y)]
    grd_all = [grd_own] + [shift(grd_own, "y", j) for j in range(1, n_y)]

    def by_block(parts):
        cut = [part.reshape(2 * n_x, 1, n_tok // (2 * n_x), width) for part in parts]
        return jnp.concatenate(cut, axis=1).reshape(n_y * n_tok, width)

    n_rows = n_exp * CAP
    recv = recv.reshape(n_exp * 2 * CAP, width)
    row_order = own_blocks(n_rows)
    spot_in = (row_order // CAP) * (2 * CAP) + row_order % CAP
    rows_in = dot(one_hot(spot_in, 2 * n_rows), recv).astype(BF16)
    rows_grad = dot(one_hot(spot_in + CAP, 2 * n_rows), recv).astype(BF16)
    part = jnp.concatenate(
        [dot(rows_in, w_gate[0]), dot(rows_in, w_up[0]), dot_cols(rows_grad, w_down[0])], axis=1
    )
    total = reduce_rows(part)
    products = jnp.concatenate(
        hidden_products(total[:, :hid], total[:, hid : 2 * hid], total[:, 2 * hid :]), axis=1
    )

    group_in, group_grad = by_block(tok_all), by_block(grd_all)
    all_w = all_w.reshape(n_z, 3, units, width)
    sh = n_z * units
    whole = [all_w[:, k].reshape(sh, width) for k in range(3)]
    shared_part = jnp.concatenate(
        [dot_cols(group_in, whole[0]), dot_cols(group_in, whole[1]), dot_cols(group_grad, whole[2])], axis=1
    )
    shared_total = reduce_rows(shared_part)
    shared_products = jnp.concatenate(
        hidden_products(shared_total[:, :sh], shared_total[:, sh : 2 * sh], shared_total[:, 2 * sh :]), axis=1
    )

    products = gather_rows(products)
    activated, grad_gate_pre, grad_up_pre = (products[:, k * hid : (k + 1) * hid] for k in range(3))
    back = dot_cols(grad_gate_pre, w_gate[0]) + dot_cols(grad_up_pre, w_up[0])
    back_natural = dot_rows(one_hot(row_order, n_rows), back.astype(BF16)).astype(BF16)
    back_rows = lax.all_to_all(
        back_natural.reshape(n_exp, CAP, width), ("z", "y"), split_axis=0, concat_axis=0, tiled=True
    )

    shared_products = gather_rows(shared_products)
    s_act, s_gate, s_up = (shared_products[:, k * sh : (k + 1) * sh] for k in range(3))
    shared_back = dot(s_gate, whole[0]) + dot(s_up, whole[1])
    shared_back = shared_back.reshape(2 * n_x, n_y, n_tok // (2 * n_x), width)
    mine = shared_back[:, 0].reshape(n_tok, width)
    for j in range(1, n_y):
        mine = mine + shift(shared_back[:, j].astype(BF16).reshape(n_tok, width), "y", -j).astype(F32)
    own = jnp.stack([dot_rows(s_gate, group_in), dot_rows(s_up, group_in), dot_rows(s_act, group_grad)])
    own = (own * scale).reshape(3, n_z, units, width).transpose(1, 0, 2, 3).reshape(n_z * 3 * units, width)
    own = lax.psum_scatter(own, "z", scatter_dimension=0, tiled=True).reshape(3, units, width)

    grad_gate = (dot_rows(rows_in, grad_gate_pre) * scale).astype(BF16)[None]
    grad_up = (dot_rows(rows_in, grad_up_pre) * scale).astype(BF16)[None]
    grad_down = (dot_rows(activated, rows_grad) * scale).astype(BF16)[None]

    place_own = dot(tok_perm, place_bf.reshape(n_tok, n_rows)).astype(BF16)
    routed = dot(place_own, back_rows.reshape(n_rows, width))
    grad_tokens = dot_rows(tok_perm, (mine + routed).astype(BF16)).astype(BF16)
    return (grad_tokens, grad_gate, grad_up, grad_down, own[0].T, own[1].T, own[2])


def solution(mesh):
    n_dp, n_expert = mesh.devices.shape
    fine = Mesh(mesh.devices.reshape(n_dp // 2, 2, n_expert // NY, NY), ("x", "core", "z", "y"))
    dp, ex = ("x", "core"), ("z", "y")
    in_specs = (
        P(ex, dp), P(ex, dp), P(ex, None), P(ex, None), P(ex, dp, None), P(ex, dp, None), P(ex, None, dp),
        P(dp, ex), P(dp, ex), P(ex, dp),
    )
    out_specs = (P(ex, dp), P(ex, dp, None), P(ex, dp, None), P(ex, None, dp), P(dp, ex), P(dp, ex), P(ex, dp))
    return jax.shard_map(shards, mesh=fine, in_specs=in_specs, out_specs=out_specs, check_vma=False)
```

```python
import jax
import jax.numpy as jnp
from jax import lax
from jax.experimental import pallas as pl
from jax.experimental.pallas import tpu as pltpu
from jax.sharding import Mesh
from jax.sharding import PartitionSpec as P

CAP = 12
NY = 4
BF16 = jnp.bfloat16
F32 = jnp.float32


def silu_parts(pre):
    sigmoid_val = jax.nn.sigmoid(pre)
    return (pre * sigmoid_val, sigmoid_val * (1.0 + pre * (1.0 - sigmoid_val)))


def dot_rows(left, right):
    return lax.dot_general(left, right, (((0,), (0,)), ((), ())), preferred_element_type=F32)


def dot_cols(left, right):
    return lax.dot_general(left, right, (((1,), (1,)), ((), ())), preferred_element_type=F32)


def dot(left, right):
    return jnp.dot(left, right, preferred_element_type=F32)


def hidden_products(part_gate, part_up, part_act):
    silu_val, silu_slope = silu_parts(part_gate)
    activated = (silu_val * part_up).astype(BF16)
    grad_gate_pre = (part_act * part_up * silu_slope).astype(BF16)
    grad_up_pre = (part_act * silu_val).astype(BF16)
    return (activated, grad_gate_pre, grad_up_pre)


def shift(value, axis, by):
    size = lax.axis_size(axis)
    return lax.ppermute(value, axis, [(i, (i + by) % size) for i in range(size)])


def pick(value, index, axis):
    return lax.dynamic_index_in_dim(value, index, axis, keepdims=False)


def x_pieces(kept, got):
    n_x, x = lax.axis_size("x"), lax.axis_index("x")
    summed = (kept + got.astype(F32)).reshape(n_x, kept.shape[0] // n_x, kept.shape[1])
    return pick(summed, x, 0), [pick(summed, (x + j) & (n_x - 1), 0).astype(BF16) for j in range(1, n_x)]


def x_sum(own, pieces):
    for j, piece in enumerate(pieces):
        own = own + shift(piece, "x", j + 1).astype(F32)
    return own


def gather_blocks(value, along=()):
    n_x = lax.axis_size("x")
    mine = [value] + [shift(value, "x", -j) for j in range(1, n_x)]
    mine[2], along = lax.optimization_barrier((mine[2], along))
    return mine + [shift(block, "core", 1) for block in mine], along


def place_kernel(where, *refs):
    *blocks, out = refs
    n_core, n_x = out.shape[:2]
    for i, block in enumerate(blocks):
        out[(where[1] + i // n_x) & (n_core - 1), (where[0] + i % n_x) & (n_x - 1)] = block[...]


def place_blocks(blocks, where):
    n_x = lax.axis_size("x")
    rows, cols = blocks[0].shape
    out = pl.pallas_call(
        place_kernel,
        out_shape=jax.ShapeDtypeStruct((2, n_x, rows, cols), blocks[0].dtype),
        in_specs=[pl.BlockSpec(memory_space=pltpu.SMEM)] + [pl.BlockSpec(memory_space=pltpu.VMEM)] * len(blocks),
        out_specs=pl.BlockSpec(memory_space=pltpu.VMEM),
        compiler_params=pltpu.CompilerParams(vmem_limit_bytes=2 << 20),
        cost_estimate=pl.CostEstimate(flops=0, bytes_accessed=8 * n_x * rows * cols, transcendentals=0),
        name="place_blocks",
    )(where, *blocks)
    return out.reshape(2 * n_x * rows, cols)


def part_kernel(where, tok, grd, weights, send, kept):
    step = pl.program_id(0)
    units = weights.shape[1] // 3
    width = weights.shape[2]
    sh = weights.shape[0] * units
    gate, up, down = (weights[:, k * units : (k + 1) * units].reshape(sh, width) for k in range(3))
    part = [dot_cols(tok[0, 0], gate), dot_cols(tok[0, 0], up), dot_cols(grd[0, 0], down)]

    @pl.when(step < 2)
    def _():
        for k in range(3):
            send[:, k * sh : (k + 1) * sh] = part[k].astype(BF16)

    @pl.when(step >= 2)
    def _():
        for k in range(3):
            kept[:, k * sh : (k + 1) * sh] = part[k]


def shared_partials(where, group, weights):
    n_y, _, n_tok, width = group.shape
    cols = weights.shape[0] * weights.shape[1]
    rows = [
        pl.BlockSpec((1, 1, n_tok, width), lambda i, where, k=k: ((i + 2 * (1 - where[1])) & 3, k, 0, 0)) for k in (0, 1)
    ]
    return pl.pallas_call(
        part_kernel,
        out_shape=(
            jax.ShapeDtypeStruct((2 * n_tok, cols), BF16),
            jax.ShapeDtypeStruct((2 * n_tok, cols), F32),
        ),
        grid_spec=pltpu.PrefetchScalarGridSpec(
            num_scalar_prefetch=1,
            grid=(n_y,),
            in_specs=[*rows, pl.BlockSpec(weights.shape, lambda i, where: (0, 0, 0), pipeline_mode=pl.Buffered(1))],
            out_specs=[
                pl.BlockSpec((n_tok, cols), lambda i, where: (jnp.minimum(i, 1), 0)),
                pl.BlockSpec((n_tok, cols), lambda i, where: (jnp.maximum(i - 2, 0), 0)),
            ],
        ),
        compiler_params=pltpu.CompilerParams(vmem_limit_bytes=11 << 20),
        cost_estimate=pl.CostEstimate(
            flops=2 * n_y * n_tok * width * cols, bytes_accessed=4 * n_y * n_tok * width, transcendentals=0
        ),
        name="shared_partials",
    )(where, group, group, weights)


def back_kernel(scale, products, tok, grd, weights, mine, back, own):
    step = pl.program_id(0)
    nz, units, width = weights.shape[0], weights.shape[1] // 3, weights.shape[2]
    sh = nz * units
    gate, up = (weights[:, k * units : (k + 1) * units].reshape(sh, width) for k in range(2))
    act, d_gate, d_up = (products[:, k * sh : (k + 1) * sh] for k in range(3))
    total = dot(d_gate, gate) + dot(d_up, up)
    back[0] = total.astype(BF16)

    @pl.when(step == 0)
    def _():
        mine[...] = total

    grads = [dot_rows(d_gate, tok[0, 0]), dot_rows(d_up, tok[0, 0]), dot_rows(act, grd[0, 0])]

    @pl.when(step == 0)
    def _():
        for k in range(3):
            own[:, k * units : (k + 1) * units] = (grads[k] * scale).reshape(nz, units, width)

    @pl.when(step > 0)
    def _():
        for k in range(3):
            own[:, k * units : (k + 1) * units] += (grads[k] * scale).reshape(nz, units, width)


def shared_back(products, group, weights, scale):
    n_y, _, n_tok, width = group.shape
    rows = [pl.BlockSpec((1, 1, n_tok, width), lambda i, k=k: (i, k, 0, 0)) for k in (0, 1)]
    whole = pl.BlockSpec(weights.shape, lambda i: (0, 0, 0), pipeline_mode=pl.Buffered(1))
    cols = products.shape[1]
    return pl.pallas_call(
        lambda *refs: back_kernel(scale, *refs),
        out_shape=(
            jax.ShapeDtypeStruct((n_tok, width), F32),
            jax.ShapeDtypeStruct((n_y, n_tok, width), BF16),
            jax.ShapeDtypeStruct(weights.shape, F32),
        ),
        grid=(n_y,),
        in_specs=[pl.BlockSpec((n_tok, cols), lambda i: (i, 0)), *rows, whole],
        out_specs=[pl.BlockSpec((n_tok, width), lambda i: (0, 0), pipeline_mode=pl.Buffered(1)), pl.BlockSpec((1, n_tok, width), lambda i: (i, 0, 0)), whole],
        compiler_params=pltpu.CompilerParams(vmem_limit_bytes=16 << 20),
        cost_estimate=pl.CostEstimate(
            flops=10 * n_y * n_tok * width * cols // 3, bytes_accessed=8 * n_y * n_tok * width, transcendentals=0
        ),
        name="shared_back",
    )(products, group, group, weights)


def routed_kernel(where, compact, recv, w_gate, w_up, w_down, rows, send, kept):
    step = pl.program_id(0)
    n_rows, tile = rows.shape[0] // 2, w_gate.shape[2]
    half = n_rows // 2
    hid = send.shape[1] // 3

    @pl.when(step == 0)
    def _():
        rows[...] = dot(compact[...], recv[...]).astype(BF16)

    def ordered(base):
        return jnp.concatenate(
            [
                rows[pl.ds(pl.multiple_of(base + (1 - where[1]) * half, half), half)],
                rows[pl.ds(pl.multiple_of(base + where[1] * half, half), half)],
            ],
            axis=0,
        )

    rows_in, rows_grad = ordered(0), ordered(n_rows)
    part = [dot(rows_in, w_gate[0]), dot(rows_in, w_up[0]), dot_cols(rows_grad, w_down[0])]
    for k in range(3):
        spot = pl.ds(pl.multiple_of(k * hid + step * tile, tile), tile)
        send[:, spot] = part[k][:half].astype(BF16)
        kept[:, spot] = part[k][half:]


def routed_partials(where, compact, recv, w_gate, w_up, w_down):
    n_rows = recv.shape[0] // 2
    width, hid = w_gate.shape[1:]
    tile = min(256, hid)
    whole = lambda shape: pl.BlockSpec(shape, lambda i, where: (0,) * len(shape), pipeline_mode=pl.Buffered(1))
    out = [
        jax.ShapeDtypeStruct((2 * n_rows, width), BF16),
        jax.ShapeDtypeStruct((n_rows // 2, 3 * hid), BF16),
        jax.ShapeDtypeStruct((n_rows // 2, 3 * hid), F32),
    ]
    return pl.pallas_call(
        routed_kernel,
        out_shape=out,
        grid_spec=pltpu.PrefetchScalarGridSpec(
            num_scalar_prefetch=1,
            grid=(hid // tile,),
            in_specs=[
                whole(compact.shape),
                whole(recv.shape),
                pl.BlockSpec((1, width, tile), lambda i, where: (0, 0, i)),
                pl.BlockSpec((1, width, tile), lambda i, where: (0, 0, i)),
                pl.BlockSpec((1, tile, width), lambda i, where: (0, i, 0)),
            ],
            out_specs=[whole(o.shape) for o in out],
        ),
        compiler_params=pltpu.CompilerParams(vmem_limit_bytes=14 << 20),
        cost_estimate=pl.CostEstimate(
            flops=6 * n_rows * width * hid, bytes_accessed=6 * width * hid, transcendentals=0
        ),
        name="routed_partials",
    )(where, compact, recv, w_gate, w_up, w_down)


def shards(tokens, grad_out, route_ids, route_gates, w_gate, w_up, w_down, shared_gate, shared_up, shared_down):
    n_z, n_y, n_x = lax.axis_size("z"), lax.axis_size("y"), lax.axis_size("x")
    n_exp = n_z * n_y
    scale = 1.0 / n_exp
    n_tok, width = tokens.shape
    hid = w_gate.shape[2]
    units = shared_down.shape[0]
    sh = n_z * units
    n_rows = n_exp * CAP

    own_w = jnp.concatenate([shared_gate.T, shared_up.T, shared_down], axis=0)
    all_w = lax.all_gather(own_w, "z", axis=0, tiled=True)

    both = jnp.stack([tokens, grad_out])
    up, down = shift(both, "y", 1), shift(both, "y", -1)

    experts = jnp.arange(n_exp, dtype=jnp.int32)[:, None]
    ids, gates = route_ids.T, route_gates.T
    chosen = jnp.zeros((n_exp, n_tok), jnp.bool_)
    gate_total = jnp.zeros((n_exp, n_tok), F32)
    for k in range(ids.shape[0]):
        match = ids[k : k + 1] == experts
        chosen = chosen | match
        gate_total = gate_total + jnp.where(match, gates[k : k + 1], 0.0)
    spots = jnp.arange(n_tok, dtype=jnp.int32)
    earlier = (spots[:, None] < spots[None, :]).astype(BF16)
    rank = dot(chosen.astype(BF16), earlier)
    rank = jnp.where(chosen, rank, -1.0)
    slots = jnp.arange(2 * CAP, dtype=jnp.int32)[None, :, None]
    rank_in = jnp.where(slots < CAP, rank.astype(jnp.int32)[:, None, :], -1) == slots
    rank_grad = jnp.where(slots >= CAP, rank.astype(jnp.int32)[:, None, :] + CAP, -1) == slots
    rank_grad = rank_grad & chosen[:, None, :]
    slot_gate = jnp.sum(jnp.where(rank_grad, gate_total[:, None, :], 0.0), axis=2)
    slot_gate = jnp.where(slots[0, :, 0][None, :] < CAP, 1.0, slot_gate)
    picked = dot(rank_in.astype(BF16).reshape(2 * n_rows, n_tok), tokens)
    picked = picked + dot(rank_grad.astype(BF16).reshape(2 * n_rows, n_tok), grad_out)
    send = (picked.reshape(n_exp, 2 * CAP, width) * slot_gate[:, :, None]).astype(BF16)
    send, up, down, _ = lax.optimization_barrier((send, up, down, own_w))
    recv = lax.all_to_all(send, ("z", "y"), split_axis=0, concat_axis=0, tiled=True)

    where = jnp.stack([lax.axis_index("x"), lax.axis_index("core")]).astype(jnp.int32)
    spot = jnp.arange(2 * n_rows, dtype=jnp.int32)
    spot = (spot % n_rows) // CAP * (2 * CAP) + spot % CAP + spot // n_rows * CAP
    compact = (spot[:, None] == jnp.arange(2 * n_rows, dtype=jnp.int32)[None, :]).astype(BF16)
    compact = lax.optimization_barrier(compact)

    all_w = all_w.reshape(n_z, 3 * units, width)
    far = n_tok // 2
    group = jnp.zeros((n_y,) + both.shape, BF16)
    for i, part in ((0, both), (1, up), (n_y - 1, down)):
        group = lax.dynamic_update_slice(group, part[None], (i, 0, 0, 0))
    group = lax.dynamic_update_slice(group, shift(up[:, :far], "y", 1)[None], (2, 0, 0, 0))
    group = lax.dynamic_update_slice(group, shift(down[:, far:], "y", -1)[None], (2, 0, far, 0))
    s_send, s_kept = shared_partials(where, group, all_w)
    s_own, s_pieces = x_pieces(s_kept, shift(s_send, "core", 1))
    rows_all, r_send, r_kept = routed_partials(
        where, compact, recv.reshape(2 * n_rows, width), w_gate, w_up, w_down
    )
    rows_in, rows_grad = rows_all[:n_rows], rows_all[n_rows:]
    r_own, r_pieces = x_pieces(r_kept, shift(r_send, "core", 1))
    s_total = x_sum(s_own, s_pieces)
    s_total, *r_pieces = lax.optimization_barrier((s_total, *r_pieces))
    s_blocks, _ = gather_blocks(
        jnp.concatenate(hidden_products(s_total[:, :sh], s_total[:, sh : 2 * sh], s_total[:, 2 * sh :]), axis=1)
    )
    r_total = x_sum(r_own, r_pieces)
    r_products = jnp.concatenate(
        hidden_products(r_total[:, :hid], r_total[:, hid : 2 * hid], r_total[:, 2 * hid :]), axis=1
    )

    s_products, r_products = lax.optimization_barrier((place_blocks(s_blocks, where), r_products))
    mine, s_back, own = shared_back(s_products, group, all_w, scale)
    y_got = [shift(s_back[j], "y", -j) for j in range(1, n_y)]
    r_blocks, y_got = gather_blocks(r_products, y_got)
    for got in y_got:
        mine = mine + got.astype(F32)
    own = lax.psum_scatter(own.reshape(n_z * 3 * units, width), "z", scatter_dimension=0, tiled=True)
    own = own.reshape(3, units, width)

    products = place_blocks(r_blocks, where)
    r_act, r_gate, r_up = (products[:, k * hid : (k + 1) * hid] for k in range(3))
    back = (dot_cols(r_gate, w_gate[0]) + dot_cols(r_up, w_up[0])).astype(BF16)
    back_rows = lax.all_to_all(
        back.reshape(n_exp, CAP, width), ("z", "y"), split_axis=0, concat_axis=0, tiled=True
    )
    grad_gate = (dot_rows(rows_in, r_gate) * scale).astype(BF16)[None]
    grad_up = (dot_rows(rows_in, r_up) * scale).astype(BF16)[None]
    grad_down = (dot_rows(r_act, rows_grad) * scale).astype(BF16)[None]

    rows = jnp.arange(n_rows, dtype=jnp.int32)[:, None]
    spread = (rows // CAP == experts[:, 0][None, :]).astype(BF16)
    placed = (dot(spread, rank.astype(BF16)).astype(jnp.int32) == rows % CAP).astype(BF16)
    routed = dot_rows(placed, back_rows.reshape(n_rows, width))
    grad_tokens = (mine + routed).astype(BF16)
    return (grad_tokens, grad_gate, grad_up, grad_down, own[0].T, own[1].T, own[2])


def solution(mesh):
    n_dp, n_expert = mesh.devices.shape
    fine = Mesh(mesh.devices.reshape(n_dp // 2, 2, n_expert // NY, NY), ("x", "core", "z", "y"))
    dp, ex = ("x", "core"), ("z", "y")
    in_specs = (
        P(ex, dp), P(ex, dp), P(ex, None), P(ex, None), P(ex, dp, None), P(ex, dp, None), P(ex, None, dp),
        P(dp, ex), P(dp, ex), P(ex, dp),
    )
    out_specs = (P(ex, dp), P(ex, dp, None), P(ex, dp, None), P(ex, None, dp), P(dp, ex), P(dp, ex), P(ex, dp))
    return jax.shard_map(shards, mesh=fine, in_specs=in_specs, out_specs=out_specs, check_vma=False)
```

```python
import jax
import jax.numpy as jnp
from jax import lax
from jax.experimental import pallas as pl
from jax.experimental.pallas import tpu as pltpu
from jax.sharding import Mesh
from jax.sharding import PartitionSpec as P

CAP = 12
NY = 4
BF16 = jnp.bfloat16
F32 = jnp.float32


def silu_parts(pre):
    sigmoid_val = jax.nn.sigmoid(pre)
    return (pre * sigmoid_val, sigmoid_val * (1.0 + pre * (1.0 - sigmoid_val)))


def dot_rows(left, right):
    return lax.dot_general(left, right, (((0,), (0,)), ((), ())), preferred_element_type=F32)


def dot_cols(left, right):
    return lax.dot_general(left, right, (((1,), (1,)), ((), ())), preferred_element_type=F32)


def dot(left, right):
    return jnp.dot(left, right, preferred_element_type=F32)


def hidden_products(part_gate, part_up, part_act):
    silu_val, silu_slope = silu_parts(part_gate)
    activated = (silu_val * part_up).astype(BF16)
    grad_gate_pre = (part_act * part_up * silu_slope).astype(BF16)
    grad_up_pre = (part_act * silu_val).astype(BF16)
    return (activated, grad_gate_pre, grad_up_pre)


def shift(value, axis, by):
    size = lax.axis_size(axis)
    return lax.ppermute(value, axis, [(i, (i + by) % size) for i in range(size)])


def pick(value, index, axis):
    return lax.dynamic_index_in_dim(value, index, axis, keepdims=False)


VMEM = pl.BlockSpec(memory_space=pltpu.VMEM)
SMEM = pl.BlockSpec(memory_space=pltpu.SMEM)
SMALL = pltpu.CompilerParams(vmem_limit_bytes=2 << 20)


def piece_kernel(where, kept, got, own, *pieces):
    block = own.shape[0]
    n_x = len(pieces) + 1
    for j in range(n_x):
        rows = pl.ds(pl.multiple_of(((where[0] + j) & (n_x - 1)) * block, block), block)
        summed = kept[rows, :] + got[rows, :].astype(F32)
        if j == 0:
            own[...] = summed
        else:
            pieces[j - 1][...] = summed.astype(BF16)


def x_pieces(where, kept, got):
    n_x = lax.axis_size("x")
    block, cols = kept.shape[0] // n_x, kept.shape[1]
    own, *pieces = pl.pallas_call(
        piece_kernel,
        out_shape=[jax.ShapeDtypeStruct((block, cols), F32)]
        + [jax.ShapeDtypeStruct((block, cols), BF16)] * (n_x - 1),
        in_specs=[SMEM, VMEM, VMEM],
        out_specs=[VMEM] * n_x,
        compiler_params=SMALL,
        cost_estimate=pl.CostEstimate(flops=n_x * block * cols, bytes_accessed=8 * n_x * block * cols, transcendentals=0),
        name="x_pieces",
    )(where, kept, got)
    return own, pieces


def act_kernel(own, *refs):
    *got, out = refs
    cols = own.shape[1] // 3
    sums = []
    for k in range(3):
        spot = slice(k * cols, (k + 1) * cols)
        total = own[:, spot].astype(F32)
        for piece in got:
            total = total + piece[:, spot].astype(F32)
        sums.append(total)
    for k, value in enumerate(hidden_products(*sums)):
        out[:, k * cols : (k + 1) * cols] = value


def x_exchange(pieces):
    return [shift(piece, "x", j + 1) for j, piece in enumerate(pieces)]


def x_products(own, got):
    return pl.pallas_call(
        act_kernel,
        out_shape=jax.ShapeDtypeStruct(own.shape, BF16),
        in_specs=[VMEM] * (1 + len(got)),
        out_specs=VMEM,
        compiler_params=SMALL,
        cost_estimate=pl.CostEstimate(flops=10 * own.size, bytes_accessed=12 * own.size, transcendentals=own.size),
        name="x_products",
    )(own, *got)


def x_blocks(value):
    return [value] + [shift(value, "x", -j) for j in range(1, lax.axis_size("x"))]


def both_cores(blocks):
    return blocks + [shift(block, "core", 1) for block in blocks]


def place_kernel(where, *refs):
    *blocks, out = refs
    n_core, n_x = out.shape[:2]
    for i, block in enumerate(blocks):
        out[(where[1] + i // n_x) & (n_core - 1), (where[0] + i % n_x) & (n_x - 1)] = block[...]


def place_blocks(blocks, where):
    n_x = lax.axis_size("x")
    rows, cols = blocks[0].shape
    out = pl.pallas_call(
        place_kernel,
        out_shape=jax.ShapeDtypeStruct((2, n_x, rows, cols), blocks[0].dtype),
        in_specs=[pl.BlockSpec(memory_space=pltpu.SMEM)] + [pl.BlockSpec(memory_space=pltpu.VMEM)] * len(blocks),
        out_specs=pl.BlockSpec(memory_space=pltpu.VMEM),
        compiler_params=pltpu.CompilerParams(vmem_limit_bytes=2 << 20),
        cost_estimate=pl.CostEstimate(flops=0, bytes_accessed=8 * n_x * rows * cols, transcendentals=0),
        name="place_blocks",
    )(where, *blocks)
    return out.reshape(2 * n_x * rows, cols)


def part_kernel(where, tok, grd, weights, send, kept):
    step = pl.program_id(0)
    units = weights.shape[1] // 3
    width = weights.shape[2]
    sh = weights.shape[0] * units
    gate, up, down = (weights[:, k * units : (k + 1) * units].reshape(sh, width) for k in range(3))
    n_tok = tok.shape[1]
    part = [dot_cols(tok[0], gate), dot_cols(tok[0], up), dot_cols(grd[0], down)]

    @pl.when(step < 2)
    def _():
        for k in range(3):
            send[pl.ds(pl.multiple_of(step * n_tok, n_tok), n_tok), k * sh : (k + 1) * sh] = part[k].astype(BF16)

    @pl.when(step >= 2)
    def _():
        for k in range(3):
            kept[pl.ds(pl.multiple_of((step - 2) * n_tok, n_tok), n_tok), k * sh : (k + 1) * sh] = part[k]


def shared_partials(where, tok, grd, weights):
    n_y, n_tok, width = tok.shape
    cols = weights.shape[0] * weights.shape[1]
    rows = pl.BlockSpec((1, n_tok, width), lambda i, where: ((i + 2 * (1 - where[1])) & 3, 0, 0))
    return pl.pallas_call(
        part_kernel,
        out_shape=(
            jax.ShapeDtypeStruct((2 * n_tok, cols), BF16),
            jax.ShapeDtypeStruct((2 * n_tok, cols), F32),
        ),
        grid_spec=pltpu.PrefetchScalarGridSpec(
            num_scalar_prefetch=1,
            grid=(n_y,),
            in_specs=[rows, rows, pl.BlockSpec(weights.shape, lambda i, where: (0, 0, 0), pipeline_mode=pl.Buffered(1))],
            out_specs=[VMEM, VMEM],
        ),
        compiler_params=pltpu.CompilerParams(vmem_limit_bytes=11 << 20),
        cost_estimate=pl.CostEstimate(
            flops=2 * n_y * n_tok * width * cols, bytes_accessed=4 * n_y * n_tok * width, transcendentals=0
        ),
        name="shared_partials",
    )(where, *(pltpu.with_memory_space_constraint(v, pltpu.HBM) for v in (tok, grd, weights)))


def back_kernel(scale, products, tok, grd, weights, mine, back, own, total_own):
    step = pl.program_id(0)
    nz, units, width = weights.shape[0], weights.shape[1] // 3, weights.shape[2]
    sh = nz * units
    gate, up = (weights[:, k * units : (k + 1) * units].reshape(sh, width) for k in range(2))
    n_tok = tok.shape[1]
    spot = pl.ds(pl.multiple_of(step * n_tok, n_tok), n_tok)
    act, d_gate, d_up = (products[spot, k * sh : (k + 1) * sh] for k in range(3))
    total = dot(d_gate, gate) + dot(d_up, up)
    back[step] = total.astype(BF16)

    @pl.when(step == 0)
    def _():
        mine[...] = total

    grads = [dot_rows(d_gate, tok[0]), dot_rows(d_up, tok[0]), dot_rows(act, grd[0])]

    @pl.when(step == 0)
    def _():
        for k in range(3):
            total_own[:, k * units : (k + 1) * units] = (grads[k] * scale).reshape(nz, units, width)

    @pl.when(step > 0)
    def _():
        for k in range(3):
            total_own[:, k * units : (k + 1) * units] += (grads[k] * scale).reshape(nz, units, width)

    @pl.when(step == pl.num_programs(0) - 1)
    def _():
        own[...] = total_own[...].astype(BF16)


def shared_back(products, tok, grd, weights, scale):
    n_y, n_tok, width = tok.shape
    rows = pl.BlockSpec((1, n_tok, width), lambda i: (i, 0, 0))
    whole = pl.BlockSpec(weights.shape, lambda i: (0, 0, 0), pipeline_mode=pl.Buffered(1))
    cols = products.shape[1]
    return pl.pallas_call(
        lambda *refs: back_kernel(scale, *refs),
        out_shape=(
            jax.ShapeDtypeStruct((n_tok, width), F32),
            jax.ShapeDtypeStruct((n_y, n_tok, width), BF16),
            jax.ShapeDtypeStruct(weights.shape, BF16),
        ),
        grid=(n_y,),
        scratch_shapes=[pltpu.VMEM(weights.shape, F32)],
        in_specs=[VMEM, rows, rows, whole],
        out_specs=[VMEM, VMEM, whole],
        compiler_params=pltpu.CompilerParams(vmem_limit_bytes=16 << 20),
        cost_estimate=pl.CostEstimate(
            flops=10 * n_y * n_tok * width * cols // 3, bytes_accessed=8 * n_y * n_tok * width, transcendentals=0
        ),
        name="shared_back",
    )(products, *(pltpu.with_memory_space_constraint(v, pltpu.HBM) for v in (tok, grd, weights)))


def routed_kernel(where, compact, recv, w_gate, w_up, w_down, rows, send, kept):
    step = pl.program_id(0)
    n_rows, tile = rows.shape[0] // 2, w_gate.shape[2]
    half = n_rows // 2
    hid = send.shape[1] // 3

    @pl.when(step == 0)
    def _():
        rows[...] = dot(compact[...], recv[...]).astype(BF16)

    def ordered(base):
        return jnp.concatenate(
            [
                rows[pl.ds(pl.multiple_of(base + (1 - where[1]) * half, half), half)],
                rows[pl.ds(pl.multiple_of(base + where[1] * half, half), half)],
            ],
            axis=0,
        )

    rows_in, rows_grad = ordered(0), ordered(n_rows)
    part = [dot(rows_in, w_gate[0]), dot(rows_in, w_up[0]), dot_cols(rows_grad, w_down[0])]
    for k in range(3):
        spot = pl.ds(pl.multiple_of(k * hid + step * tile, tile), tile)
        send[:, spot] = part[k][:half].astype(BF16)
        kept[:, spot] = part[k][half:]


def routed_partials(where, compact, recv, w_gate, w_up, w_down):
    n_rows = recv.shape[0] // 2
    width, hid = w_gate.shape[1:]
    tile = min(256, hid)
    out = [
        jax.ShapeDtypeStruct((2 * n_rows, width), BF16),
        jax.ShapeDtypeStruct((n_rows // 2, 3 * hid), BF16),
        jax.ShapeDtypeStruct((n_rows // 2, 3 * hid), F32),
    ]
    return pl.pallas_call(
        routed_kernel,
        out_shape=out,
        grid_spec=pltpu.PrefetchScalarGridSpec(
            num_scalar_prefetch=1,
            grid=(hid // tile,),
            in_specs=[
                VMEM,
                VMEM,
                pl.BlockSpec((1, width, tile), lambda i, where: (0, 0, i)),
                pl.BlockSpec((1, width, tile), lambda i, where: (0, 0, i)),
                pl.BlockSpec((1, tile, width), lambda i, where: (0, i, 0)),
            ],
            out_specs=[VMEM] * 3,
        ),
        compiler_params=pltpu.CompilerParams(vmem_limit_bytes=14 << 20),
        cost_estimate=pl.CostEstimate(
            flops=6 * n_rows * width * hid, bytes_accessed=6 * width * hid, transcendentals=0
        ),
        name="routed_partials",
    )(where, compact, recv, *(pltpu.with_memory_space_constraint(w, pltpu.HBM) for w in (w_gate, w_up, w_down)))


def shards(tokens, grad_out, route_ids, route_gates, w_gate, w_up, w_down, shared_gate, shared_up, shared_down):
    n_z, n_y, n_x = lax.axis_size("z"), lax.axis_size("y"), lax.axis_size("x")
    n_exp = n_z * n_y
    scale = 1.0 / n_exp
    n_tok, width = tokens.shape
    hid = w_gate.shape[2]
    units = shared_down.shape[0]
    sh = n_z * units
    n_rows = n_exp * CAP

    own_w = jnp.concatenate([shared_gate.T, shared_up.T, shared_down], axis=0)

    tokens, grad_out, own_w = lax.optimization_barrier((tokens, grad_out, own_w))
    all_w = lax.all_gather(own_w, "z", axis=0, tiled=True)
    tok_up, tok_down = shift(tokens, "y", 1), shift(tokens, "y", -1)
    grd_up, grd_down = shift(grad_out, "y", 1), shift(grad_out, "y", -1)

    experts = jnp.arange(n_exp, dtype=jnp.int32)[:, None]
    ids, gates = route_ids.T, route_gates.T
    chosen = jnp.zeros((n_exp, n_tok), jnp.bool_)
    gate_total = jnp.zeros((n_exp, n_tok), F32)
    for k in range(ids.shape[0]):
        match = ids[k : k + 1] == experts
        chosen = chosen | match
        gate_total = gate_total + jnp.where(match, gates[k : k + 1], 0.0)
    spots = jnp.arange(n_tok, dtype=jnp.int32)
    earlier = (spots[:, None] < spots[None, :]).astype(BF16)
    rank = dot(chosen.astype(BF16), earlier)
    rank = jnp.where(chosen, rank, -1.0)
    slots = jnp.arange(2 * CAP, dtype=jnp.int32)[None, :, None]
    rank_in = jnp.where(slots < CAP, rank.astype(jnp.int32)[:, None, :], -1) == slots
    rank_grad = jnp.where(slots >= CAP, rank.astype(jnp.int32)[:, None, :] + CAP, -1) == slots
    rank_grad = rank_grad & chosen[:, None, :]
    slot_gate = jnp.sum(jnp.where(rank_grad, gate_total[:, None, :], 0.0), axis=2)
    slot_gate = jnp.where(slots[0, :, 0][None, :] < CAP, 1.0, slot_gate)
    picked = dot(rank_in.astype(BF16).reshape(2 * n_rows, n_tok), tokens)
    picked = picked + dot(rank_grad.astype(BF16).reshape(2 * n_rows, n_tok), grad_out)
    send = (picked.reshape(n_exp, 2 * CAP, width) * slot_gate[:, :, None]).astype(BF16)
    where = jnp.stack([lax.axis_index("x"), lax.axis_index("core")]).astype(jnp.int32)
    spot = jnp.arange(2 * n_rows, dtype=jnp.int32)
    spot = (spot % n_rows) // CAP * (2 * CAP) + spot % CAP + spot // n_rows * CAP
    compact = (spot[:, None] == jnp.arange(2 * n_rows, dtype=jnp.int32)[None, :]).astype(BF16)
    rows = jnp.arange(n_rows, dtype=jnp.int32)[:, None]
    spread = (rows // CAP == experts[:, 0][None, :]).astype(BF16)
    placed = (dot(spread, rank.astype(BF16)).astype(jnp.int32) == rows % CAP).astype(BF16)

    far = n_tok // 2
    tok_beyond = [shift(tok_up[:far], "y", 1), shift(tok_down[far:], "y", -1)]
    grd_beyond = [shift(grd_up[:far], "y", 1), shift(grd_down[far:], "y", -1)]
    send, tok_beyond, where, compact, placed, _ = lax.optimization_barrier(
        (send, tok_beyond, where, compact, placed, own_w)
    )
    recv = lax.all_to_all(send, ("z", "y"), split_axis=0, concat_axis=0, tiled=True)
    groups = []
    for own_rows, up, down, beyond in (
        (tokens, tok_up, tok_down, tok_beyond),
        (grad_out, grd_up, grd_down, grd_beyond),
    ):
        group = jnp.zeros((n_y, n_tok, width), BF16)
        for i, start, part in ((0, 0, own_rows), (1, 0, up), (n_y - 1, 0, down), (2, 0, beyond[0]), (2, far, beyond[1])):
            group = lax.dynamic_update_slice(group, part[None], (i, start, 0))
        groups.append(group)
    group_in, group_grad = groups

    all_w = all_w.reshape(n_z, 3 * units, width)
    s_send, s_kept = shared_partials(where, group_in, group_grad, all_w)
    s_own, s_pieces = x_pieces(where, s_kept, shift(s_send, "core", 1))
    s_mine = x_products(s_own, x_exchange(s_pieces))
    s_products = lax.all_gather(s_mine, ("core", "x"), axis=0, tiled=True)
    recv, _ = lax.optimization_barrier((recv, s_mine))
    rows_all, r_send, r_kept = routed_partials(
        where, compact, recv.reshape(2 * n_rows, width), w_gate, w_up, w_down
    )
    rows_in, rows_grad = rows_all[:n_rows], rows_all[n_rows:]
    r_own, r_pieces = x_pieces(where, r_kept, shift(r_send, "core", 1))

    r_mine = x_products(r_own, x_exchange(r_pieces))
    s_products, r_mine = lax.optimization_barrier((s_products, r_mine))
    mine, s_back, own = shared_back(s_products, group_in, group_grad, all_w, scale)
    r_blocks = x_blocks(r_mine)
    y_got = [shift(s_back[j], "y", -j) for j in range(1, n_y)]
    for got in y_got:
        mine = mine + got.astype(F32)
    own = lax.psum_scatter(own.reshape(n_z * 3 * units, width), "z", scatter_dimension=0, tiled=True)
    own = own.astype(F32).reshape(3, units, width)

    products = place_blocks(both_cores(r_blocks), where)
    r_act, r_gate, r_up = (products[:, k * hid : (k + 1) * hid] for k in range(3))
    back = (dot_cols(r_gate, w_gate[0]) + dot_cols(r_up, w_up[0])).astype(BF16)
    back_rows = lax.all_to_all(
        back.reshape(n_exp, CAP, width), ("z", "y"), split_axis=0, concat_axis=0, tiled=True
    )
    back_rows, *own = lax.optimization_barrier((back_rows, own[0].T, own[1].T, own[2]))
    products, _ = lax.optimization_barrier((products, y_got))
    r_act, r_gate, r_up = (products[:, k * hid : (k + 1) * hid] for k in range(3))
    grad_gate = (dot_rows(rows_in, r_gate) * scale).astype(BF16)[None]
    grad_up = (dot_rows(rows_in, r_up) * scale).astype(BF16)[None]
    grad_down = (dot_rows(r_act, rows_grad) * scale).astype(BF16)[None]

    routed = dot_rows(placed, back_rows.reshape(n_rows, width))
    grad_tokens = (mine + routed).astype(BF16)
    return (grad_tokens, grad_gate, grad_up, grad_down, *own)


def solution(mesh):
    n_dp, n_expert = mesh.devices.shape
    fine = Mesh(mesh.devices.reshape(n_dp // 2, 2, n_expert // NY, NY), ("x", "core", "z", "y"))
    dp, ex = ("x", "core"), ("z", "y")
    in_specs = (
        P(ex, dp), P(ex, dp), P(ex, None), P(ex, None), P(ex, dp, None), P(ex, dp, None), P(ex, None, dp),
        P(dp, ex), P(dp, ex), P(ex, dp),
    )
    out_specs = (P(ex, dp), P(ex, dp, None), P(ex, dp, None), P(ex, None, dp), P(dp, ex), P(dp, ex), P(ex, dp))
    return jax.shard_map(shards, mesh=fine, in_specs=in_specs, out_specs=out_specs, check_vma=False)
```

```python
import jax
import jax.numpy as jnp
from jax import lax
from jax.experimental import pallas as pl
from jax.experimental.pallas import tpu as pltpu
from jax.sharding import Mesh
from jax.sharding import PartitionSpec as P

CAP = 12
NY = 4
BF16 = jnp.bfloat16
F32 = jnp.float32


def silu_parts(pre):
    sigmoid_val = jax.nn.sigmoid(pre)
    return (pre * sigmoid_val, sigmoid_val * (1.0 + pre * (1.0 - sigmoid_val)))


def dot_rows(left, right):
    return lax.dot_general(left, right, (((0,), (0,)), ((), ())), preferred_element_type=F32)


def dot_cols(left, right):
    return lax.dot_general(left, right, (((1,), (1,)), ((), ())), preferred_element_type=F32)


def dot(left, right):
    return jnp.dot(left, right, preferred_element_type=F32)


def hidden_products(part_gate, part_up, part_act):
    silu_val, silu_slope = silu_parts(part_gate)
    activated = (silu_val * part_up).astype(BF16)
    grad_gate_pre = (part_act * part_up * silu_slope).astype(BF16)
    grad_up_pre = (part_act * silu_val).astype(BF16)
    return (activated, grad_gate_pre, grad_up_pre)


def shift(value, axis, by):
    size = lax.axis_size(axis)
    return lax.ppermute(value, axis, [(i, (i + by) % size) for i in range(size)])


def pick(value, index, axis):
    return lax.dynamic_index_in_dim(value, index, axis, keepdims=False)


VMEM = pl.BlockSpec(memory_space=pltpu.VMEM)
SMEM = pl.BlockSpec(memory_space=pltpu.SMEM)
SMALL = pltpu.CompilerParams(vmem_limit_bytes=2 << 20)


def piece_kernel(where, kept, got, own, *pieces):
    block = own.shape[0]
    n_x = len(pieces) + 1
    for j in range(n_x):
        rows = pl.ds(pl.multiple_of(((where[0] + j) & (n_x - 1)) * block, block), block)
        summed = kept[rows, :] + got[rows, :].astype(F32)
        if j == 0:
            own[...] = summed
        else:
            pieces[j - 1][...] = summed.astype(BF16)


def x_pieces(where, kept, got):
    n_x = lax.axis_size("x")
    block, cols = kept.shape[0] // n_x, kept.shape[1]
    own, *pieces = pl.pallas_call(
        piece_kernel,
        out_shape=[jax.ShapeDtypeStruct((block, cols), F32)]
        + [jax.ShapeDtypeStruct((block, cols), BF16)] * (n_x - 1),
        in_specs=[SMEM, VMEM, VMEM],
        out_specs=[VMEM] * n_x,
        compiler_params=SMALL,
        cost_estimate=pl.CostEstimate(flops=n_x * block * cols, bytes_accessed=8 * n_x * block * cols, transcendentals=0),
        name="x_pieces",
    )(where, kept, got)
    return own, pieces


def act_kernel(own, *refs):
    *got, out = refs
    cols = own.shape[1] // 3
    sums = []
    for k in range(3):
        spot = slice(k * cols, (k + 1) * cols)
        total = own[:, spot].astype(F32)
        for piece in got:
            total = total + piece[:, spot].astype(F32)
        sums.append(total)
    for k, value in enumerate(hidden_products(*sums)):
        out[:, k * cols : (k + 1) * cols] = value


def x_exchange(pieces):
    return [shift(piece, "x", j + 1) for j, piece in enumerate(pieces)]


def x_products(own, got):
    return pl.pallas_call(
        act_kernel,
        out_shape=jax.ShapeDtypeStruct(own.shape, BF16),
        in_specs=[VMEM] * (1 + len(got)),
        out_specs=VMEM,
        compiler_params=SMALL,
        cost_estimate=pl.CostEstimate(flops=10 * own.size, bytes_accessed=12 * own.size, transcendentals=own.size),
        name="x_products",
    )(own, *got)


def x_blocks(value):
    return [value] + [shift(value, "x", -j) for j in range(1, lax.axis_size("x"))]


def both_cores(blocks):
    return blocks + [shift(block, "core", 1) for block in blocks]


def place_kernel(where, *refs):
    *blocks, out = refs
    n_core, n_x = out.shape[:2]
    for i, block in enumerate(blocks):
        out[(where[1] + i // n_x) & (n_core - 1), (where[0] + i % n_x) & (n_x - 1)] = block[...]


def place_blocks(blocks, where):
    n_x = lax.axis_size("x")
    rows, cols = blocks[0].shape
    out = pl.pallas_call(
        place_kernel,
        out_shape=jax.ShapeDtypeStruct((2, n_x, rows, cols), blocks[0].dtype),
        in_specs=[pl.BlockSpec(memory_space=pltpu.SMEM)] + [pl.BlockSpec(memory_space=pltpu.VMEM)] * len(blocks),
        out_specs=pl.BlockSpec(memory_space=pltpu.VMEM),
        compiler_params=pltpu.CompilerParams(vmem_limit_bytes=2 << 20),
        cost_estimate=pl.CostEstimate(flops=0, bytes_accessed=8 * n_x * rows * cols, transcendentals=0),
        name="place_blocks",
    )(where, *blocks)
    return out.reshape(2 * n_x * rows, cols)


def part_kernel(where, tok, grd, weights, send, kept):
    step = pl.program_id(0)
    units = weights.shape[1] // 3
    width = weights.shape[2]
    sh = weights.shape[0] * units
    gate, up, down = (weights[:, k * units : (k + 1) * units].reshape(sh, width) for k in range(3))
    n_tok = tok.shape[1]
    part = [dot_cols(tok[0], gate), dot_cols(tok[0], up), dot_cols(grd[0], down)]

    @pl.when(step < 2)
    def _():
        for k in range(3):
            send[pl.ds(pl.multiple_of(step * n_tok, n_tok), n_tok), k * sh : (k + 1) * sh] = part[k].astype(BF16)

    @pl.when(step >= 2)
    def _():
        for k in range(3):
            kept[pl.ds(pl.multiple_of((step - 2) * n_tok, n_tok), n_tok), k * sh : (k + 1) * sh] = part[k]


def shared_partials(where, tok, grd, weights):
    n_y, n_tok, width = tok.shape
    cols = weights.shape[0] * weights.shape[1]
    rows = pl.BlockSpec((1, n_tok, width), lambda i, where: ((i + 2 * (1 - where[1])) & 3, 0, 0))
    return pl.pallas_call(
        part_kernel,
        out_shape=(
            jax.ShapeDtypeStruct((2 * n_tok, cols), BF16),
            jax.ShapeDtypeStruct((2 * n_tok, cols), F32),
        ),
        grid_spec=pltpu.PrefetchScalarGridSpec(
            num_scalar_prefetch=1,
            grid=(n_y,),
            in_specs=[rows, rows, pl.BlockSpec(weights.shape, lambda i, where: (0, 0, 0), pipeline_mode=pl.Buffered(1))],
            out_specs=[VMEM, VMEM],
        ),
        compiler_params=pltpu.CompilerParams(vmem_limit_bytes=11 << 20),
        cost_estimate=pl.CostEstimate(
            flops=2 * n_y * n_tok * width * cols, bytes_accessed=4 * n_y * n_tok * width, transcendentals=0
        ),
        name="shared_partials",
    )(where, *(pltpu.with_memory_space_constraint(v, pltpu.HBM) for v in (tok, grd, weights)))


def back_kernel(scale, products, tok, grd, weights, mine, back, own, total_own):
    step = pl.program_id(0)
    nz, units, width = weights.shape[0], weights.shape[1] // 3, weights.shape[2]
    sh = nz * units
    gate, up = (weights[:, k * units : (k + 1) * units].reshape(sh, width) for k in range(2))
    act, d_gate, d_up = (products[:, k * sh : (k + 1) * sh] for k in range(3))
    total = dot(d_gate, gate) + dot(d_up, up)
    back[step] = total.astype(BF16)

    @pl.when(step == 0)
    def _():
        mine[...] = total

    grads = [dot_rows(d_gate, tok[0]), dot_rows(d_up, tok[0]), dot_rows(act, grd[0])]

    @pl.when(step == 0)
    def _():
        for k in range(3):
            total_own[:, k * units : (k + 1) * units] = (grads[k] * scale).reshape(nz, units, width)

    @pl.when(step > 0)
    def _():
        for k in range(3):
            total_own[:, k * units : (k + 1) * units] += (grads[k] * scale).reshape(nz, units, width)

    @pl.when(step == pl.num_programs(0) - 1)
    def _():
        own[...] = total_own[...].astype(BF16)


def shared_back(products, tok, grd, weights, scale):
    n_y, n_tok, width = tok.shape
    rows = pl.BlockSpec((1, n_tok, width), lambda i: (i, 0, 0))
    whole = pl.BlockSpec(weights.shape, lambda i: (0, 0, 0), pipeline_mode=pl.Buffered(1))
    cols = products.shape[1]
    return pl.pallas_call(
        lambda *refs: back_kernel(scale, *refs),
        out_shape=(
            jax.ShapeDtypeStruct((n_tok, width), F32),
            jax.ShapeDtypeStruct((n_y, n_tok, width), BF16),
            jax.ShapeDtypeStruct(weights.shape, BF16),
        ),
        grid=(n_y,),
        scratch_shapes=[pltpu.VMEM(weights.shape, F32)],
        in_specs=[pl.BlockSpec((n_tok, cols), lambda i: (i, 0)), rows, rows, whole],
        out_specs=[VMEM, VMEM, whole],
        compiler_params=pltpu.CompilerParams(vmem_limit_bytes=16 << 20),
        cost_estimate=pl.CostEstimate(
            flops=10 * n_y * n_tok * width * cols // 3, bytes_accessed=8 * n_y * n_tok * width, transcendentals=0
        ),
        name="shared_back",
    )(*(pltpu.with_memory_space_constraint(v, pltpu.HBM) for v in (products, tok, grd, weights)))


def routed_kernel(where, compact, recv, w_gate, w_up, w_down, rows, send, kept, ordered):
    step = pl.program_id(0)
    n_rows, tile = rows.shape[0] // 2, w_gate.shape[2]
    half = n_rows // 2
    hid = send.shape[1] // 3

    @pl.when(step == 0)
    def _():
        rows[...] = dot(compact[...], recv[...]).astype(BF16)
        for base in (0, n_rows):
            for i, side in enumerate((1 - where[1], where[1])):
                source = pl.ds(pl.multiple_of(base + side * half, half), half)
                ordered[base + i * half : base + (i + 1) * half, :] = rows[source, :]

    rows_in, rows_grad = ordered[:n_rows, :], ordered[n_rows:, :]
    part = [dot(rows_in, w_gate[0]), dot(rows_in, w_up[0]), dot_cols(rows_grad, w_down[0])]
    for k in range(3):
        spot = pl.ds(pl.multiple_of(k * hid + step * tile, tile), tile)
        send[:, spot] = part[k][:half].astype(BF16)
        kept[:, spot] = part[k][half:]


def routed_partials(where, compact, recv, w_gate, w_up, w_down):
    n_rows = recv.shape[0] // 2
    width, hid = w_gate.shape[1:]
    tile = min(512, hid)
    out = [
        jax.ShapeDtypeStruct((2 * n_rows, width), BF16),
        jax.ShapeDtypeStruct((n_rows // 2, 3 * hid), BF16),
        jax.ShapeDtypeStruct((n_rows // 2, 3 * hid), F32),
    ]
    return pl.pallas_call(
        routed_kernel,
        out_shape=out,
        grid_spec=pltpu.PrefetchScalarGridSpec(
            num_scalar_prefetch=1,
            grid=(hid // tile,),
            in_specs=[
                VMEM,
                VMEM,
                pl.BlockSpec((1, width, tile), lambda i, where: (0, 0, i)),
                pl.BlockSpec((1, width, tile), lambda i, where: (0, 0, i)),
                pl.BlockSpec((1, tile, width), lambda i, where: (0, i, 0)),
            ],
            out_specs=[VMEM] * 3,
            scratch_shapes=[pltpu.VMEM((2 * n_rows, width), BF16)],
        ),
        compiler_params=pltpu.CompilerParams(vmem_limit_bytes=14 << 20),
        cost_estimate=pl.CostEstimate(
            flops=6 * n_rows * width * hid, bytes_accessed=6 * width * hid, transcendentals=0
        ),
        name="routed_partials",
    )(where, compact, recv, *(pltpu.with_memory_space_constraint(w, pltpu.HBM) for w in (w_gate, w_up, w_down)))


def shards(tokens, grad_out, route_ids, route_gates, w_gate, w_up, w_down, shared_gate, shared_up, shared_down):
    n_z, n_y, n_x = lax.axis_size("z"), lax.axis_size("y"), lax.axis_size("x")
    n_exp = n_z * n_y
    scale = 1.0 / n_exp
    n_tok, width = tokens.shape
    hid = w_gate.shape[2]
    units = shared_down.shape[0]
    sh = n_z * units
    n_rows = n_exp * CAP

    own_w = jnp.concatenate([shared_gate.T, shared_up.T, shared_down], axis=0)

    tokens, grad_out, own_w = lax.optimization_barrier((tokens, grad_out, own_w))
    all_w = lax.all_gather(own_w, "z", axis=0, tiled=True)
    tok_up, tok_down = shift(tokens, "y", 1), shift(tokens, "y", -1)
    grd_up, grd_down = shift(grad_out, "y", 1), shift(grad_out, "y", -1)

    experts = jnp.arange(n_exp, dtype=jnp.int32)[:, None]
    ids, gates = route_ids.T, route_gates.T
    chosen = jnp.zeros((n_exp, n_tok), jnp.bool_)
    gate_total = jnp.zeros((n_exp, n_tok), F32)
    for k in range(ids.shape[0]):
        match = ids[k : k + 1] == experts
        chosen = chosen | match
        gate_total = gate_total + jnp.where(match, gates[k : k + 1], 0.0)
    spots = jnp.arange(n_tok, dtype=jnp.int32)
    earlier = (spots[:, None] < spots[None, :]).astype(BF16)
    rank = dot(chosen.astype(BF16), earlier)
    rank = jnp.where(chosen, rank, -1.0)
    slots = jnp.arange(2 * CAP, dtype=jnp.int32)[None, :, None]
    rank_in = jnp.where(slots < CAP, rank.astype(jnp.int32)[:, None, :], -1) == slots
    rank_grad = jnp.where(slots >= CAP, rank.astype(jnp.int32)[:, None, :] + CAP, -1) == slots
    rank_grad = rank_grad & chosen[:, None, :]
    slot_gate = jnp.sum(jnp.where(rank_grad, gate_total[:, None, :], 0.0), axis=2)
    slot_gate = jnp.where(slots[0, :, 0][None, :] < CAP, 1.0, slot_gate)
    picked = dot(rank_in.astype(BF16).reshape(2 * n_rows, n_tok), tokens)
    picked = picked + dot(rank_grad.astype(BF16).reshape(2 * n_rows, n_tok), grad_out)
    send = (picked.reshape(n_exp, 2 * CAP, width) * slot_gate[:, :, None]).astype(BF16)
    where = jnp.stack([lax.axis_index("x"), lax.axis_index("core")]).astype(jnp.int32)
    spot = jnp.arange(2 * n_rows, dtype=jnp.int32)
    spot = (spot % n_rows) // CAP * (2 * CAP) + spot % CAP + spot // n_rows * CAP
    compact = (spot[:, None] == jnp.arange(2 * n_rows, dtype=jnp.int32)[None, :]).astype(BF16)
    rows = jnp.arange(n_rows, dtype=jnp.int32)[:, None]
    spread = (rows // CAP == experts[:, 0][None, :]).astype(BF16)
    placed = (dot(spread, rank.astype(BF16)).astype(jnp.int32) == rows % CAP).astype(BF16)

    far = n_tok // 2
    tok_beyond = [shift(tok_up[:far], "y", 1), shift(tok_down[far:], "y", -1)]
    grd_beyond = [shift(grd_up[:far], "y", 1), shift(grd_down[far:], "y", -1)]
    send, tok_beyond, where, compact, placed, _ = lax.optimization_barrier(
        (send, tok_beyond, where, compact, placed, own_w)
    )
    recv = lax.all_to_all(send, ("z", "y"), split_axis=0, concat_axis=0, tiled=True)
    groups = []
    for own_rows, up, down, beyond in (
        (tokens, tok_up, tok_down, tok_beyond),
        (grad_out, grd_up, grd_down, grd_beyond),
    ):
        group = jnp.zeros((n_y, n_tok, width), BF16)
        for i, start, part in ((0, 0, own_rows), (1, 0, up), (n_y - 1, 0, down), (2, 0, beyond[0]), (2, far, beyond[1])):
            group = lax.dynamic_update_slice(group, part[None], (i, start, 0))
        groups.append(group)
    group_in, group_grad = groups

    all_w = all_w.reshape(n_z, 3 * units, width)
    s_send, s_kept = shared_partials(where, group_in, group_grad, all_w)
    s_own, s_pieces = x_pieces(where, s_kept, shift(s_send, "core", 1))
    s_mine = x_products(s_own, x_exchange(s_pieces))
    s_products = lax.all_gather(s_mine, ("core", "x"), axis=0, tiled=True)
    recv, _ = lax.optimization_barrier((recv, s_mine))
    rows_all, r_send, r_kept = routed_partials(
        where, compact, recv.reshape(2 * n_rows, width), w_gate, w_up, w_down
    )
    rows_in, rows_grad = rows_all[:n_rows], rows_all[n_rows:]
    r_own, r_pieces = x_pieces(where, r_kept, shift(r_send, "core", 1))

    r_mine = x_products(r_own, x_exchange(r_pieces))
    s_products, r_mine = lax.optimization_barrier((s_products, r_mine))
    mine, s_back, own = shared_back(s_products, group_in, group_grad, all_w, scale)
    r_blocks = x_blocks(r_mine)
    y_got = [shift(s_back[j], "y", -j) for j in range(1, n_y)]
    for got in y_got:
        mine = mine + got.astype(F32)
    own = lax.psum_scatter(own.reshape(n_z * 3 * units, width), "z", scatter_dimension=0, tiled=True)
    own = own.astype(F32).reshape(3, units, width)

    products = place_blocks(both_cores(r_blocks), where)
    r_act, r_gate, r_up = (products[:, k * hid : (k + 1) * hid] for k in range(3))
    back = (dot_cols(r_gate, w_gate[0]) + dot_cols(r_up, w_up[0])).astype(BF16)
    back_rows = lax.all_to_all(
        back.reshape(n_exp, CAP, width), ("z", "y"), split_axis=0, concat_axis=0, tiled=True
    )
    back_rows, *own = lax.optimization_barrier((back_rows, own[0].T, own[1].T, own[2]))
    products, _ = lax.optimization_barrier((products, y_got))
    r_act, r_gate, r_up = (products[:, k * hid : (k + 1) * hid] for k in range(3))
    grad_gate = (dot_rows(rows_in, r_gate) * scale).astype(BF16)[None]
    grad_up = (dot_rows(rows_in, r_up) * scale).astype(BF16)[None]
    grad_down = (dot_rows(r_act, rows_grad) * scale).astype(BF16)[None]

    routed = dot_rows(placed, back_rows.reshape(n_rows, width))
    grad_tokens = (mine + routed).astype(BF16)
    return (grad_tokens, grad_gate, grad_up, grad_down, *own)


def solution(mesh):
    n_dp, n_expert = mesh.devices.shape
    fine = Mesh(mesh.devices.reshape(n_dp // 2, 2, n_expert // NY, NY), ("x", "core", "z", "y"))
    dp, ex = ("x", "core"), ("z", "y")
    in_specs = (
        P(ex, dp), P(ex, dp), P(ex, None), P(ex, None), P(ex, dp, None), P(ex, dp, None), P(ex, None, dp),
        P(dp, ex), P(dp, ex), P(ex, dp),
    )
    out_specs = (P(ex, dp), P(ex, dp, None), P(ex, dp, None), P(ex, None, dp), P(dp, ex), P(dp, ex), P(ex, dp))
    return jax.shard_map(shards, mesh=fine, in_specs=in_specs, out_specs=out_specs, check_vma=False)
```
